32 devices in a mesh: row: 8 (over z, core), col: 4 (over y, x).
Axes of the slice: x: 2, y: 2, z: 4, core: 2. Of those that a mesh axis runs over, the one named last changes fastest.
Arguments:
- amplitudes: bfloat16 [16, 16, 800, 800], P('col', None, 'row'), as said below
- integrals: bfloat16 [16, 16, 800, 800], P('col', None, 'row'), may hold values from -6 to 6
- fock_virtual: bfloat16 [800, 800], replicated, may hold values from -0.21875 to 0.21875
- occ_levels: int32 [16], replicated, may hold values from -12 to -3
- vir_levels: int32 [800], replicated, may hold values from 2 to 21
- ladder_ints: bfloat16 [800, 800, 2, 800], P('row', 'col'), may hold values from -0.0078125 to 0.0078125
Outputs:
- new_amps: bfloat16 [16, 16, 800, 800], P('col', None, 'row')
- ladder: bfloat16 [16, 16, 2, 800], P('col', 'row')
The draws below stay inside these ranges and needn't reach their ends.
Inputs may be any that keep to these rules, and one draw needn't show every extreme that they name: amplitudes[i, j, a, b] equals amplitudes[j, i, b, a] exactly.
All inputs are finite; a program needn't handle non-finite values.
Results may differ from the reference program's by a relative error of at most 0.0049.
Values may be sent and summed in bfloat16 or wider, within the bound.
A program may use at most 384 MiB of HBM per device.

```python
import jax
import jax.numpy as jnp
from jax import lax

OCCUPIED = 16
VIRTUAL = 800
WINDOW = 2


def draw_amplitudes(key, part):
    sample = jax.random.normal(key, (OCCUPIED, OCCUPIED, VIRTUAL, VIRTUAL), jnp.float32)
    return ((sample + jnp.transpose(sample, (1, 0, 3, 2))) * 0.7071).astype(jnp.bfloat16)


def touch_ends(array, stream_key, low, top_value):
    place = [jax.random.randint(jax.random.fold_in(stream_key, axis), (), 0, length) for axis, length in enumerate(array.shape)]
    main_axis = array.shape.index(max(array.shape))
    beside = place[:main_axis] + [(place[main_axis] + 1) % array.shape[main_axis]] + place[main_axis + 1:]
    return array.at[tuple(place)].set(low).at[tuple(beside)].set(top_value)


def block_scale(rng, shape, cuts, least, top_value):
    level = 1.0
    for position, parts in cuts:
        heights = jax.random.uniform(jax.random.fold_in(jax.random.fold_in(rng, 6), position), (parts,), jnp.float32, least / len(cuts), top_value / len(cuts))
        level = level * jnp.repeat(jnp.exp(heights), shape[position] // parts).reshape((-1,) + (1,) * (len(shape) - 1 - position))
    return level


def normal_values(stream_key, dims, spread, bound, pieces=(), held_as=jnp.bfloat16):
    entries = jax.random.normal(stream_key, dims, jnp.float32) * spread
    if len(pieces) > 0:
        entries = block_scale(stream_key, dims, pieces, -0.22, 0.18) * entries
    return jnp.clip(entries, min=-bound, max=bound).astype(held_as)


def setup_inputs(seed: int = 0) -> dict:
    streams_of = jax.random.split(jax.random.key(seed), 7)
    return {
        "amplitudes": draw_amplitudes(jax.random.fold_in(streams_of[6], 71), 0),
        "integrals": normal_values(streams_of[1], (OCCUPIED, OCCUPIED, VIRTUAL, VIRTUAL), 1.0, 6.0, ((0, 4), (2, 8))),
        "fock_virtual": normal_values(streams_of[2], (VIRTUAL, VIRTUAL), VIRTUAL ** -0.5, 0.21875),
        "occ_levels": touch_ends(jax.random.randint(streams_of[3], (OCCUPIED,), -12, -2), jax.random.fold_in(streams_of[3], 1), -12, (-2) - 1).astype(jnp.int32),
        "vir_levels": touch_ends(jax.random.randint(streams_of[4], (VIRTUAL,), 2, 22), jax.random.fold_in(streams_of[4], 1), 2, 21).astype(jnp.int32),
        "ladder_ints": normal_values(streams_of[5], (VIRTUAL, VIRTUAL, WINDOW, VIRTUAL), (VIRTUAL * VIRTUAL) ** -0.5, 0.0078125, ((0, 8), (1, 4))),
    }


level_step = 0.1


def reference(amplitudes, integrals, fock_virtual, occ_levels, vir_levels, ladder_ints):
    amp_float = amplitudes.astype(jnp.float32)
    fock_float = fock_virtual.astype(jnp.float32)
    left_term = jnp.einsum('ac,ijcb->ijab', fock_float, amp_float)
    right_term = jnp.einsum('ijac,bc->ijab', amp_float, fock_float)
    dressed = integrals.astype(jnp.float32) + left_term + right_term
    summed = dressed + jnp.transpose(dressed, (1, 0, 3, 2))
    level_sum = vir_levels[None, None, :, None] + vir_levels[None, None, None, :] - occ_levels[:, None, None, None] - occ_levels[None, :, None, None]
    denom = level_sum.astype(jnp.float32) * level_step
    new_amps = (summed / denom).astype(jnp.bfloat16)
    flat_amps = jnp.moveaxis(new_amps.reshape(OCCUPIED * OCCUPIED, VIRTUAL, VIRTUAL), 1, 0)

    def accumulate(running, inputs):
        amp_rows, integral_rows = inputs
        weights = integral_rows.reshape(VIRTUAL, WINDOW * VIRTUAL)
        return running + jnp.dot(amp_rows, weights, preferred_element_type=jnp.float32), None

    initial = jnp.zeros((OCCUPIED * OCCUPIED, WINDOW * VIRTUAL), jnp.float32)
    running, unused = lax.scan(accumulate, initial, (flat_amps, ladder_ints))
    ladder = running.reshape(OCCUPIED, OCCUPIED, WINDOW, VIRTUAL).astype(jnp.bfloat16)
    return new_amps, ladder
```

```python
import functools

import jax
import jax.numpy as jnp
from jax import lax
from jax.experimental import pallas as pl
from jax.experimental.pallas import tpu as pltpu
from jax.sharding import PartitionSpec as P

level_step = 0.1
MESH = pl.DeviceIdType.MESH


def exchange_kernel(rows, cols, src, dst, send_sem, recv_sem, local_sem):
    count = rows * cols
    me = lax.axis_index("row") * cols + lax.axis_index("col")
    barrier = pltpu.get_barrier_semaphore()

    def place(number):
        return (number // cols, number % cols)

    def greet(k, carry):
        peer = lax.rem(me + k, count)
        pl.semaphore_signal(barrier, inc=1, device_id=place(peer), device_id_type=MESH)
        return carry

    lax.fori_loop(1, count, greet, 0)
    pl.semaphore_wait(barrier, count - 1)
    own = pltpu.make_async_copy(src.at[me], dst.at[me], local_sem)
    own.start()

    def copy_to(k):
        peer = lax.rem(me + k, count)
        return pltpu.make_async_remote_copy(
            src_ref=src.at[peer],
            dst_ref=dst.at[me],
            send_sem=send_sem.at[k - 1],
            recv_sem=recv_sem.at[k - 1],
            device_id=place(peer),
            device_id_type=MESH,
        )

    def begin(k, carry):
        copy_to(k).start()
        return carry

    def finish(k, carry):
        copy_to(k).wait()
        return carry

    lax.fori_loop(1, count, begin, 0)
    lax.fori_loop(1, count, finish, 0)
    own.wait()


def exchange(blocks, rows, cols, number):
    count = rows * cols
    return pl.pallas_call(
        functools.partial(exchange_kernel, rows, cols),
        out_shape=jax.ShapeDtypeStruct(blocks.shape, blocks.dtype),
        in_specs=[pl.BlockSpec(memory_space=pl.ANY)],
        out_specs=pl.BlockSpec(memory_space=pl.ANY),
        scratch_shapes=[
            pltpu.SemaphoreType.DMA((count - 1,)),
            pltpu.SemaphoreType.DMA((count - 1,)),
            pltpu.SemaphoreType.DMA,
        ],
        compiler_params=pltpu.CompilerParams(collective_id=number, has_side_effects=True),
    )(blocks)


def wire_shape(elements):
    lanes = 128
    while elements % lanes:
        lanes //= 2
    return (elements // lanes, lanes)


def mirror_pairs(sent, rows, cols):
    occ_block, occ_all, vir_block, vir_all = sent.shape
    count = rows * cols
    split = sent.reshape(occ_block, cols, occ_block, vir_block, rows, vir_block)
    blocks = jnp.transpose(split, (4, 1, 2, 5, 0, 3))
    elements = blocks.size // count
    received = exchange(blocks.reshape((count,) + wire_shape(elements)), rows, cols, 0)
    received = received.reshape(rows, cols, occ_block, vir_block, occ_block, vir_block)
    return jnp.transpose(received, (2, 1, 4, 3, 0, 5)).reshape(sent.shape)


def body(rows, cols, amplitudes, integrals, fock_virtual, occ_levels, vir_levels, ladder_ints):
    occ_block, occ_all, vir_block, vir_all = amplitudes.shape
    right_term = jnp.einsum(
        "ijac,bc->ijab", amplitudes, fock_virtual, preferred_element_type=jnp.float32
    )
    dressed = integrals.astype(jnp.float32) + 2.0 * right_term
    sent = dressed.astype(jnp.bfloat16)
    summed = dressed + mirror_pairs(sent, rows, cols).astype(jnp.float32)
    occ_mine = lax.dynamic_slice_in_dim(occ_levels, lax.axis_index("col") * occ_block, occ_block, 0)
    vir_mine = lax.dynamic_slice_in_dim(vir_levels, lax.axis_index("row") * vir_block, vir_block, 0)
    level_sum = (
        vir_mine[None, None, :, None]
        + vir_levels[None, None, None, :]
        - occ_mine[:, None, None, None]
        - occ_levels[None, :, None, None]
    )
    denom = level_sum.astype(jnp.float32) * level_step
    new_amps = (summed / denom).astype(jnp.bfloat16)
    slab_rows, slab_cols, window_size, vir_width = ladder_ints.shape
    depth = slab_rows * slab_cols
    pieces = new_amps.reshape(occ_block * occ_all, vir_block, cols, slab_cols)
    pieces = jnp.transpose(pieces, (2, 0, 1, 3)).reshape(cols * occ_block * occ_all, depth)
    received = lax.all_to_all(pieces, "col", split_axis=0, concat_axis=0, tiled=True)
    terms = [
        jnp.dot(
            received,
            ladder_ints[:, :, w, :].reshape(depth, vir_width),
            preferred_element_type=jnp.float32,
        )
        for w in range(window_size)
    ]
    occ_row = occ_all // rows
    term = jnp.stack(terms, axis=1).reshape(cols, occ_block, rows, occ_row, window_size, vir_width)
    term = jnp.transpose(term, (2, 0, 1, 3, 4, 5))
    elements = term.size // (rows * cols)
    parts = exchange(term.reshape((rows * cols,) + wire_shape(elements)), rows, cols, 1)
    ladder = jnp.sum(parts, axis=0).reshape(occ_block, occ_row, window_size, vir_width)
    return (new_amps, ladder.astype(jnp.bfloat16))


def solution(mesh):
    placed = (
        P("col", None, "row", None),
        P("col", None, "row", None),
        P(),
        P(),
        P(),
        P("row", "col", None, None),
    )
    return jax.shard_map(
        functools.partial(body, mesh.shape["row"], mesh.shape["col"]),
        mesh=mesh,
        in_specs=placed,
        out_specs=(P("col", None, "row", None), P("col", "row", None, None)),
        check_vma=False,
    )
```

```python
import functools

import jax
import jax.numpy as jnp
from jax import lax
from jax.experimental import pallas as pl
from jax.experimental.pallas import tpu as pltpu
from jax.sharding import PartitionSpec as P

level_step = 0.1
MESH = pl.DeviceIdType.MESH


def exchange_kernel(rows, cols, src, dst, send_sem, recv_sem, local_sem):
    count = rows * cols
    row, col = lax.axis_index("row"), lax.axis_index("col")
    me = row * cols + col
    barrier = pltpu.get_barrier_semaphore()

    def partner(k):
        turn = k // cols
        away = rows // 2 + ((turn + 1) // 2) * (1 - 2 * (turn % 2))
        return ((row + away + rows) % rows, (col + k % cols + 1) % cols)

    def greet(k, carry):
        pl.semaphore_signal(barrier, inc=1, device_id=partner(k), device_id_type=MESH)
        return carry

    lax.fori_loop(0, count - 1, greet, 0)
    pl.semaphore_wait(barrier, count - 1)

    def copy_to(k):
        peer_row, peer_col = partner(k)
        return pltpu.make_async_remote_copy(
            src_ref=src.at[peer_row * cols + peer_col],
            dst_ref=dst.at[me],
            send_sem=send_sem.at[k],
            recv_sem=recv_sem.at[k],
            device_id=(peer_row, peer_col),
            device_id_type=MESH,
        )

    def begin(k, carry):
        copy_to(k).start()
        return carry

    def finish(k, carry):
        copy_to(k).wait()
        return carry

    lax.fori_loop(0, count - 1, begin, 0)
    own = pltpu.make_async_copy(src.at[me], dst.at[me], local_sem)
    own.start()
    lax.fori_loop(0, count - 1, finish, 0)
    own.wait()


def exchange(blocks, rows, cols, number):
    count = rows * cols
    return pl.pallas_call(
        functools.partial(exchange_kernel, rows, cols),
        out_shape=jax.ShapeDtypeStruct(blocks.shape, blocks.dtype),
        in_specs=[pl.BlockSpec(memory_space=pl.ANY)],
        out_specs=pl.BlockSpec(memory_space=pl.ANY),
        scratch_shapes=[
            pltpu.SemaphoreType.DMA((count - 1,)),
            pltpu.SemaphoreType.DMA((count - 1,)),
            pltpu.SemaphoreType.DMA,
        ],
        compiler_params=pltpu.CompilerParams(collective_id=number, has_side_effects=True),
    )(blocks)


def wire_shape(elements):
    lanes = 128
    while elements % lanes:
        lanes //= 2
    return (elements // lanes, lanes)


def mirror_pairs(sent, rows, cols):
    occ_block, occ_all, vir_block, vir_all = sent.shape
    count = rows * cols
    split = sent.reshape(occ_block, cols, occ_block, vir_block, rows, vir_block)
    blocks = jnp.transpose(split, (4, 1, 2, 5, 0, 3))
    elements = blocks.size // count
    received = exchange(blocks.reshape((count,) + wire_shape(elements)), rows, cols, 0)
    received = received.reshape(rows, cols, occ_block, vir_block, occ_block, vir_block)
    return jnp.transpose(received, (2, 1, 4, 3, 0, 5)).reshape(sent.shape)


def window_kernel(slab_ref, *out_refs):
    parted = pltpu.einshape("tab->atb", slab_ref[...])
    for number, out_ref in enumerate(out_refs):
        out_ref[...] = parted[number]


def window_weights(ladder_ints):
    slab_rows, slab_cols, window_size, vir_width = ladder_ints.shape
    depth = slab_rows * slab_cols
    tile = next((t for t in range(400, 0, -8) if depth % t == 0), depth)
    return pl.pallas_call(
        window_kernel,
        grid=(depth // tile,),
        in_specs=[pl.BlockSpec((tile, window_size, vir_width), lambda k: (k, 0, 0))],
        out_specs=[pl.BlockSpec((tile, vir_width), lambda k: (k, 0))] * window_size,
        out_shape=[jax.ShapeDtypeStruct((depth, vir_width), ladder_ints.dtype)] * window_size,
        cost_estimate=pl.CostEstimate(
            flops=0, bytes_accessed=4 * ladder_ints.size, transcendentals=0
        ),
    )(ladder_ints.reshape(depth, window_size, vir_width))


def body(rows, cols, amplitudes, integrals, fock_virtual, occ_levels, vir_levels, ladder_ints):
    occ_block, occ_all, vir_block, vir_all = amplitudes.shape
    right_term = jnp.einsum(
        "ijac,bc->ijab", amplitudes, fock_virtual, preferred_element_type=jnp.float32
    )
    dressed = integrals.astype(jnp.float32) + 2.0 * right_term
    sent = dressed.astype(jnp.bfloat16)
    mirrored = lax.optimization_barrier(mirror_pairs(sent, rows, cols))
    summed = dressed + mirrored.astype(jnp.float32)
    occ_mine = lax.dynamic_slice_in_dim(occ_levels, lax.axis_index("col") * occ_block, occ_block, 0)
    vir_mine = lax.dynamic_slice_in_dim(vir_levels, lax.axis_index("row") * vir_block, vir_block, 0)
    level_sum = (
        vir_mine[None, None, :, None]
        + vir_levels[None, None, None, :]
        - occ_mine[:, None, None, None]
        - occ_levels[None, :, None, None]
    )
    denom = level_sum.astype(jnp.float32) * level_step
    new_amps = (summed / denom).astype(jnp.bfloat16)
    slab_rows, slab_cols, window_size, vir_width = ladder_ints.shape
    depth = slab_rows * slab_cols
    pieces = new_amps.reshape(occ_block * occ_all, vir_block, cols, slab_cols)
    pieces = jnp.transpose(pieces, (2, 0, 1, 3)).reshape(cols * occ_block * occ_all, depth)
    received = lax.all_to_all(pieces, "col", split_axis=0, concat_axis=0, tiled=True)
    terms = lax.optimization_barrier(
        [
            jnp.dot(received, weights, preferred_element_type=jnp.float32)
            for weights in window_weights(ladder_ints)
        ]
    )
    occ_row = occ_all // rows
    term = jnp.stack(terms, axis=1).reshape(cols, occ_block, rows, occ_row, window_size, vir_width)
    term = jnp.transpose(term, (2, 0, 1, 3, 4, 5))
    elements = term.size // (rows * cols)
    blocks = term.astype(jnp.bfloat16).reshape((rows * cols,) + wire_shape(elements))
    parts = exchange(blocks, rows, cols, 1)
    ladder = jnp.sum(parts.astype(jnp.float32), axis=0).reshape(occ_block, occ_row, window_size, vir_width)
    return (new_amps, ladder.astype(jnp.bfloat16))


def solution(mesh):
    placed = (
        P("col", None, "row", None),
        P("col", None, "row", None),
        P(),
        P(),
        P(),
        P("row", "col", None, None),
    )
    return jax.shard_map(
        functools.partial(body, mesh.shape["row"], mesh.shape["col"]),
        mesh=mesh,
        in_specs=placed,
        out_specs=(P("col", None, "row", None), P("col", "row", None, None)),
        check_vma=False,
    )
```
